256 devices in a mesh: gx: 32 (over y, x, core), gy: 8 (over z).
Axes of the slice: x: 4, y: 4, z: 8, core: 2. Of those that a mesh axis runs over, the one named last changes fastest.
Arguments:
- operator_blocks: float32 [64, 16, 12, 7, 64, 64], P('gx', 'gy'), may hold values from -1 to 13, as said below
- start_block: float32 [64, 16, 12, 64, 16], P('gx', 'gy'), may hold values from -4000 to 4000
Outputs:
- orthonormal: float32 [64, 16, 12, 64, 80], P('gx', 'gy')
- triangle: float32 [80, 80], replicated
The draws below stay inside these ranges and needn't reach their ends.
Inputs may be any that keep to these rules, and one draw needn't show every extreme that they name: `operator_blocks`: the own block of every element is diagonally dominant; other entries are small.
All inputs are finite; a program needn't handle non-finite values.
Results may differ from the reference program's by a relative error of at most 0.0003.
Values sent between devices are 32-bit elements; how exact they have to be, the bound alone decides.
No kernel may reach another device: no remote copies, remote signals or barrier semaphores. Data moves between devices by JAX's collectives and lax.ppermute only.
A program may use at most 64 MiB of HBM per device.

```python
import jax
import jax.numpy as jnp
from jax import lax

P_SIZE = 64
RHS = 16
STEPS = 4
COLS = 80
NX = 64
NY = 16
NZ = 12


def draw_operator_blocks(key, part):
    first, second = jax.random.split(jax.random.fold_in(key, 11), 2)
    spread = 0.4 / P_SIZE ** 0.5
    noise = spread * jnp.clip(jax.random.normal(first, (NX, NY, NZ, 7, P_SIZE, P_SIZE), jnp.float32), -4.0, 4.0)
    diagonal = jax.random.uniform(second, (NX, NY, NZ, P_SIZE), jnp.float32, 4.0, 12.0)
    identity = jnp.eye(P_SIZE, dtype=jnp.float32)
    own = noise[:, :, :, 0] + diagonal[..., :, None] * identity
    return noise.at[:, :, :, 0].set(own)


def draw_start_block(key, part):
    keys = jax.random.split(jax.random.fold_in(key, 23), 3)
    logten = jnp.log(10.0)
    rows = jnp.exp(logten * jax.random.uniform(keys[1], (NX, NY, NZ, P_SIZE, 1), jnp.float32))
    columns = jnp.exp(logten * jax.random.uniform(keys[2], (RHS,), jnp.float32))
    along_x = jnp.arange(NX, dtype=jnp.float32) / max(NX - 1, 1)
    along_y = jnp.arange(NY, dtype=jnp.float32) / max(NY - 1, 1)
    trend = jnp.exp(jnp.log(3.0) * (along_x[:, None] + along_y[None, :]))
    values = jnp.clip(jax.random.normal(keys[0], (NX, NY, NZ, P_SIZE, RHS), jnp.float32), -4.0, 4.0)
    return values * rows * columns * trend[:, :, None, None, None]


def setup_inputs(seed: int = 0) -> dict:
    key_list = jax.random.split(jax.random.key(seed), 3)
    return {
        "operator_blocks": draw_operator_blocks(jax.random.fold_in(key_list[2], 71), 0),
        "start_block": draw_start_block(jax.random.fold_in(key_list[2], 71), 0),
    }


def apply_operator(vector, operator_blocks):
    padded = jnp.pad(vector, ((1, 1), (1, 1), (1, 1), (0, 0), (0, 0)))
    stacked = jnp.stack([vector, padded[:-2, 1:-1, 1:-1], padded[2:, 1:-1, 1:-1], padded[1:-1, :-2, 1:-1], padded[1:-1, 2:, 1:-1], padded[1:-1, 1:-1, :-2], padded[1:-1, 1:-1, 2:]], axis=3)
    return jnp.einsum('xyzfij,xyzfjr->xyzir', operator_blocks, stacked, precision=lax.Precision.HIGHEST)

def reference(operator_blocks, start_block):
    previous = start_block
    current = (apply_operator(previous, operator_blocks) - 8.0 * previous) / 6.0
    pieces = [previous, current]
    for index in range(STEPS - 1):
        following = 2.0 * (apply_operator(current, operator_blocks) - 8.0 * current) / 6.0 - previous
        previous, current = (current, following)
        pieces.append(following)
    basis = jnp.concatenate(pieces, axis=-1)
    tall = basis.reshape(-1, COLS)
    factor_q, factor_r = jnp.linalg.qr(tall)
    signs = jnp.where(jnp.diagonal(factor_r) >= 0, 1.0, -1.0).astype(factor_r.dtype)
    orthonormal = (factor_q * signs[None, :]).reshape(basis.shape)
    triangle = factor_r * signs[:, None]
    return (orthonormal, triangle)
```

```python
import functools

import jax
import jax.numpy as jnp
from jax import lax
from jax.experimental import pallas as pl
from jax.experimental.pallas import tpu as pltpu
from jax.sharding import PartitionSpec as P

F32 = jnp.float32
BF16 = jnp.bfloat16
Z = 12
R = 16
U = 64
L = 2 * U
FACE = Z * L
WIDE = 2 * FACE
STEPS = 4
COLS = (STEPS + 1) * R
VMEM_LIMIT = 16 * 1024 * 1024
NT = (((1,), (1,)), ((), ()))
TN = (((0,), (0,)), ((), ()))

VM = pl.BlockSpec(memory_space=pltpu.VMEM)


def low_lanes(shape):
    return lax.broadcasted_iota(jnp.int32, shape, len(shape) - 1) < U


def split(value):
    high = value.astype(BF16)
    return high, (value - high.astype(F32)).astype(BF16)


def product(left, w_high, w_low):
    high, low = split(left)
    both = lax.dot_general(
        jnp.concatenate([high, low], axis=0), w_high, NT, preferred_element_type=F32
    )
    rest = lax.dot_general(high, w_low, NT, preferred_element_type=F32)
    total = both[: 2 * R] + both[2 * R :] + rest
    return jnp.where(low_lanes((R, L)), total[:R], total[R:])


def swapped(pair):
    return pltpu.roll(pair, U, 1)


def parity():
    return lax.axis_index("gx") & 1, lax.axis_index("gy") & 1


def lanes(x, z):
    base = (x * Z + z) * L
    return slice(base, base + L)


def store_packets(pairs, px, py, e_ref, o_ref, ee_ref, oo_ref):
    low = low_lanes((R, L))
    for z in range(Z):
        at = slice(z * L, (z + 1) * L)
        first, second = pairs[0][z], pairs[1][z]
        e_ref[:, at] = jnp.where(px == 0, second, first)
        o_ref[:, at] = jnp.where(px == 0, first, second)
        face0 = jnp.where(low, first, swapped(second))
        face1 = jnp.where(low, swapped(first), second)
        ee_ref[:, at] = jnp.where(py == 0, face1, face0)
        oo_ref[:, at] = jnp.where(py == 0, face0, face1)


def begin_kernel(s_ref, p_ref, e_ref, o_ref, ee_ref, oo_ref):
    px, py = parity()
    pairs = [[None] * Z for _ in range(2)]
    for x in range(2):
        for z in range(Z):
            pair = jnp.concatenate([s_ref[x, 0, z], s_ref[x, 1, z]], axis=1)
            p_ref[:, lanes(x, z)] = pair
            pairs[x][z] = pair
    store_packets(pairs, px, py, e_ref, o_ref, ee_ref, oo_ref)


def weights_kernel(a_ref, lh_ref, ll_ref, eh_ref, el_ref):
    zero = jnp.zeros((U, U), F32)
    for x in range(2):
        for y in range(2):
            rows = slice(y * U, (y + 1) * U)
            f = lambda k: a_ref[x, y, 0, k]
            tiles = (
                (f(0), f(2 - x)),
                (f(5), f(6)),
                (f(4 - y), zero),
            )
            for t, (one, two) in enumerate(tiles):
                high, low = split(jnp.concatenate([one, two], axis=1))
                lh_ref[x, 0, rows, t * L : (t + 1) * L] = high
                ll_ref[x, 0, rows, t * L : (t + 1) * L] = low
            along_x, along_y = f(1 + x), f(3 + y)
            outer = (along_y, along_x) if x == 0 else (along_x, along_y)
            high, low = split(jnp.concatenate(outer, axis=1))
            eh_ref[x, 0, rows, :] = high
            el_ref[x, 0, rows, :] = low


def local_kernel(p_ref, lh_ref, ll_ref, out_ref):
    low = low_lanes((R, L))
    pairs = [[p_ref[:, lanes(x, z)] for z in range(Z)] for x in range(2)]
    turned = [[swapped(v) for v in row] for row in pairs]
    zero = jnp.zeros((R, L), F32)

    def at(rows, x, z):
        return rows[x][z] if 0 <= z < Z else zero

    for x in range(2):
        for z in range(Z):
            a = [
                jnp.where(low, pairs[x][z], turned[1 - x][z]),
                jnp.where(low, at(pairs, x, z - 1), at(turned, x, z + 1)),
                turned[x][z],
            ]
            b = [
                jnp.where(low, turned[x][z], pairs[1 - x][z]),
                jnp.where(low, at(turned, x, z - 1), at(pairs, x, z + 1)),
                pairs[x][z],
            ]
            left = jnp.concatenate([jnp.concatenate(a, axis=1), jnp.concatenate(b, axis=1)], axis=0)
            out_ref[:, lanes(x, z)] = product(left, lh_ref[x, z], ll_ref[x, z])


def outer_kernel(first, last, *refs):
    part_ref, p_ref = refs[:2]
    refs = refs[2:]
    if not first:
        before_ref, refs = refs[0], refs[1:]
    e_ref, o_ref, ee_ref, oo_ref, eh_ref, el_ref, *outs = refs
    px, py = parity()
    low = low_lanes((R, L))
    gx, gy = lax.axis_index("gx"), lax.axis_index("gy")
    o_there = jnp.logical_and(gx > 0, gx < lax.axis_size("gx") - 1)
    oo_there = jnp.logical_and(gy > 0, gy < lax.axis_size("gy") - 1)
    pairs = [[None] * Z for _ in range(2)]
    for z in range(Z):
        at = slice(z * L, (z + 1) * L)
        e, o, ee, oo = e_ref[:, at], o_ref[:, at], ee_ref[:, at], oo_ref[:, at]
        o = jnp.where(o_there, o, 0.0)
        oo = jnp.where(oo_there, oo, 0.0)
        x0, x1 = jnp.where(px == 0, o, e), jnp.where(px == 0, e, o)
        ym, yp = jnp.where(py == 0, oo, ee), jnp.where(py == 0, ee, oo)
        left0 = jnp.concatenate([jnp.where(low, ym, swapped(x0)), jnp.where(low, yp, x0)], axis=0)
        left1 = jnp.concatenate([jnp.where(low, x1, ym), jnp.where(low, swapped(x1), yp)], axis=0)
        for x, left in ((0, left0), (1, left1)):
            here = lanes(x, z)
            applied = part_ref[:, here] + product(left, eh_ref[x, z], el_ref[x, z])
            shifted = (applied - 8.0 * p_ref[:, here]) * (1.0 / 6.0)
            pairs[x][z] = shifted if first else 2.0 * shifted - before_ref[:, here]
            outs[0][:, here] = pairs[x][z]
    if not last:
        store_packets(pairs, px, py, *outs[1:])


def gram_kernel(*refs):
    *blocks, g_ref = refs
    tall = jnp.concatenate([b[...] for b in blocks], axis=0)
    g_ref[:, :COLS] = lax.dot_general(
        tall, tall, NT, precision=lax.Precision.HIGHEST, preferred_element_type=F32
    )
    g_ref[:, COLS:] = jnp.zeros((COLS, L - COLS), F32)


def finish_kernel(g_ref, b0, b1, b2, b3, b4, q_ref, r_ref):
    tiles = [g_ref[8 * i : 8 * i + 8, :] for i in range(COLS // 8)]
    lane = lax.broadcasted_iota(jnp.int32, (8, L), 1)
    sub = lax.broadcasted_iota(jnp.int32, (8, L), 0)
    pivots = []
    for k in range(COLS):
        t, s = divmod(k, 8)
        row = jnp.broadcast_to(tiles[t][s : s + 1, :], (8, L))
        pivot = jnp.broadcast_to(tiles[t][s : s + 1, k : k + 1], (8, L))
        pivots.append(pivot)
        scaled = row * (1.0 / pivot)
        here = lane == k
        scaled = jnp.where(here, 1.0 / pivot, scaled)
        for i in range(t, COLS // 8):
            column = jnp.broadcast_to(tiles[i][:, k : k + 1], (8, L))
            kept = jnp.where(here, 0.0, tiles[i])
            new = kept - column * scaled
            tiles[i] = new if i > t else jnp.where(sub > s, new, tiles[i])
    inverse = []
    for i in range(COLS // 8):
        pivot = pivots[8 * i]
        for s in range(1, 8):
            pivot = jnp.where(sub == s, pivots[8 * i + s], pivot)
        scale = lax.rsqrt(pivot)
        rows = tiles[i] * scale
        index = sub + 8 * i
        r_ref[8 * i : 8 * i + 8, :] = jnp.where(lane >= index, rows, 0.0)[:, :COLS]
        inverse.append(jnp.where(lane < index, rows, jnp.where(lane == index, scale, 0.0)))
    inverse = jnp.concatenate(inverse, axis=0)[:, :COLS]
    blocks = (b0, b1, b2, b3, b4)
    for x in range(2):
        for z in range(Z):
            tall = jnp.concatenate([b[:, lanes(x, z)] for b in blocks], axis=0)
            rows = jnp.transpose(
                jnp.dot(inverse, tall, precision=lax.Precision.HIGHEST, preferred_element_type=F32)
            )
            q_ref[x, 0, z] = rows[:U]
            q_ref[x, 1, z] = rows[U:]


def call(kernel, outs, n_in, **more):
    shapes = [jax.ShapeDtypeStruct(s, d) for s, d in outs]
    one = len(shapes) == 1
    return pl.pallas_call(
        kernel,
        out_shape=shapes[0] if one else shapes,
        in_specs=[VM] * n_in,
        out_specs=VM if one else [VM] * len(shapes),
        compiler_params=pltpu.CompilerParams(vmem_limit_bytes=VMEM_LIMIT),
        **more,
    )


PACKETS = [((R, FACE), F32)] * 4
BLOCK = [((R, WIDE), F32)]


def exchange(packets):
    wide = lax.axis_size("gx")
    deep = lax.axis_size("gy")

    def even(n):
        return [(i, i ^ 1) for i in range(n)]

    def odd(n):
        there = [(i, (i + 1) % n) for i in range(1, n, 2)]
        return there + [(j, i) for i, j in there]

    e, o, ee, oo = packets
    oo = lax.ppermute(oo, "gy", odd(deep))
    ee = lax.ppermute(ee, "gy", even(deep))
    o = lax.ppermute(o, "gx", odd(wide))
    e = lax.ppermute(e, "gx", even(wide))
    return e, o, ee, oo


def total_over_devices(gram):
    for axis, masks in (("gx", (1, 2, 6, 8, 24)), ("gy", (1, 2, 7))):
        count = lax.axis_size(axis)
        for mask in masks:
            gram = gram + lax.ppermute(gram, axis, [(i, i ^ mask) for i in range(count)])
    return gram


def weights(operator_blocks):
    local, outer = (2, Z, L, 3 * L), (2, Z, L, L)
    block = lambda width: pl.BlockSpec((2, 1, L, width), lambda z: (0, z, 0, 0))
    return pl.pallas_call(
        weights_kernel,
        grid=(Z,),
        out_shape=[jax.ShapeDtypeStruct(s, BF16) for s in (local, local, outer, outer)],
        in_specs=[pl.BlockSpec((2, 2, 1, 7, U, U), lambda z: (0, 0, z, 0, 0, 0))],
        out_specs=[block(3 * L), block(3 * L), block(L), block(L)],
        compiler_params=pltpu.CompilerParams(vmem_limit_bytes=VMEM_LIMIT),
    )(operator_blocks)


def per_device(operator_blocks, start_block):
    start = jnp.swapaxes(start_block, 3, 4)
    now, *packets = call(begin_kernel, BLOCK + PACKETS, 1)(start)
    arrived = exchange(packets)
    local_high, local_low, outer_high, outer_low = weights(operator_blocks)
    blocks = [now]
    for step in range(STEPS):
        first, last = step == 0, step == STEPS - 1
        part = call(local_kernel, BLOCK, 3)(blocks[-1], local_high, local_low)
        before = [] if first else [blocks[-2]]
        operands = [part, blocks[-1], *before, *arrived, outer_high, outer_low]
        outs = call(
            functools.partial(outer_kernel, first, last),
            BLOCK + ([] if last else PACKETS),
            len(operands),
        )(*operands)
        if last:
            blocks.append(outs)
        else:
            blocks.append(outs[0])
            arrived = exchange(outs[1:])
    gram = call(gram_kernel, [((COLS, L), F32)], len(blocks))(*blocks)
    gram = total_over_devices(gram)
    return call(finish_kernel, [((2, 2, Z, U, COLS), F32), ((COLS, COLS), F32)], 1 + len(blocks))(
        gram, *blocks
    )


def solution(mesh):
    in_specs = (P("gx", "gy", None, None, None, None), P("gx", "gy", None, None, None))
    out_specs = (P("gx", "gy", None, None, None), P())
    return jax.shard_map(
        per_device, mesh=mesh, in_specs=in_specs, out_specs=out_specs, check_vma=False
    )
```

```python
import functools

import jax
import jax.numpy as jnp
from jax import lax
from jax.experimental import pallas as pl
from jax.experimental.pallas import tpu as pltpu
from jax.sharding import PartitionSpec as P

F32 = jnp.float32
BF16 = jnp.bfloat16
Z = 12
R = 16
U = 64
L = 2 * U
FACE = Z * L
WIDE = 2 * FACE
STEPS = 4
COLS = (STEPS + 1) * R
VMEM_LIMIT = 16 * 1024 * 1024
NT = (((1,), (1,)), ((), ()))
TN = (((0,), (0,)), ((), ()))

VM = pl.BlockSpec(memory_space=pltpu.VMEM)


def low_lanes(shape):
    return lax.broadcasted_iota(jnp.int32, shape, len(shape) - 1) < U


def split(value):
    high = value.astype(BF16)
    return high, (value - high.astype(F32)).astype(BF16)


def product(left, w_high, w_low):
    high, low = split(left)
    both = lax.dot_general(
        jnp.concatenate([high, low], axis=0), w_high, NT, preferred_element_type=F32
    )
    rest = lax.dot_general(high, w_low, NT, preferred_element_type=F32)
    total = both[: 2 * R] + both[2 * R :] + rest
    return jnp.where(low_lanes((R, L)), total[:R], total[R:])


def swapped(pair):
    return pltpu.roll(pair, U, 1)


def parity():
    return lax.axis_index("gx") & 1, lax.axis_index("gy") & 1


def lanes(x, z):
    base = (x * Z + z) * L
    return slice(base, base + L)


def store_packets(pairs, px, py, e_ref, o_ref, ee_ref, oo_ref):
    low = low_lanes((R, L))
    for z in range(Z):
        at = slice(z * L, (z + 1) * L)
        first, second = pairs[0][z], pairs[1][z]
        e_ref[:, at] = jnp.where(px == 0, second, first)
        o_ref[:, at] = jnp.where(px == 0, first, second)
        face0 = jnp.where(low, first, swapped(second))
        face1 = jnp.where(low, swapped(first), second)
        ee_ref[:, at] = jnp.where(py == 0, face1, face0)
        oo_ref[:, at] = jnp.where(py == 0, face0, face1)


def begin_kernel(s_ref, p_ref, e_ref, o_ref, ee_ref, oo_ref):
    px, py = parity()
    pairs = [[None] * Z for _ in range(2)]
    for x in range(2):
        for z in range(Z):
            pair = jnp.concatenate([s_ref[x, 0, z], s_ref[x, 1, z]], axis=1)
            p_ref[:, lanes(x, z)] = pair
            pairs[x][z] = pair
    store_packets(pairs, px, py, e_ref, o_ref, ee_ref, oo_ref)


def neighbour_rows(p_ref):
    low = low_lanes((R, L))
    pairs = [[p_ref[:, lanes(x, z)] for z in range(Z)] for x in range(2)]
    turned = [[swapped(v) for v in row] for row in pairs]
    zero = jnp.zeros((R, L), F32)

    def at(rows, x, z):
        return rows[x][z] if 0 <= z < Z else zero

    def left(x, z):
        a = [
            jnp.where(low, pairs[x][z], turned[1 - x][z]),
            jnp.where(low, at(pairs, x, z - 1), at(turned, x, z + 1)),
            turned[x][z],
        ]
        b = [
            jnp.where(low, turned[x][z], pairs[1 - x][z]),
            jnp.where(low, at(turned, x, z - 1), at(pairs, x, z + 1)),
            pairs[x][z],
        ]
        return jnp.concatenate([jnp.concatenate(a, axis=1), jnp.concatenate(b, axis=1)], axis=0)

    return left


def gram_row(blocks):
    tall = jnp.concatenate(blocks, axis=0)
    row = lax.dot_general(
        blocks[-1], tall, NT, precision=lax.Precision.HIGHEST, preferred_element_type=F32
    )
    return jnp.concatenate([row, jnp.zeros((R, L - row.shape[1]), F32)], axis=1)


def first_kernel(a_ref, p_ref, lh_ref, ll_ref, eh_ref, el_ref, out_ref, g_ref, buffer, arrived):
    copies = [
        pltpu.make_async_copy(a_ref.at[:, :, z], buffer.at[z], arrived.at[z]) for z in range(Z)
    ]
    for copy in copies:
        copy.start()
    g_ref[...] = gram_row([p_ref[...]])
    left = neighbour_rows(p_ref)
    zero = jnp.zeros((U, U), F32)
    for z in range(Z):
        copies[z].wait()
        for x in range(2):
            for y in range(2):
                rows = slice(y * U, (y + 1) * U)
                f = [buffer[z, x, y, k] for k in range(7)]
                tiles = ((f[0], f[2 - x]), (f[5], f[6]), (f[4 - y], zero))
                for t, both in enumerate(tiles):
                    high, low = split(jnp.concatenate(both, axis=1))
                    lh_ref[x, z, rows, t * L : (t + 1) * L] = high
                    ll_ref[x, z, rows, t * L : (t + 1) * L] = low
                along_x, along_y = f[1 + x], f[3 + y]
                outer = (along_y, along_x) if x == 0 else (along_x, along_y)
                eh_ref[x, z, rows, :], el_ref[x, z, rows, :] = split(jnp.concatenate(outer, axis=1))
            out_ref[:, lanes(x, z)] = product(left(x, z), lh_ref[x, z], ll_ref[x, z])


def local_kernel(lh_ref, ll_ref, *refs):
    *blocks, out_ref, g_ref = refs
    left = neighbour_rows(blocks[-1])
    for x in range(2):
        for z in range(Z):
            out_ref[:, lanes(x, z)] = product(left(x, z), lh_ref[x, z], ll_ref[x, z])
    g_ref[...] = gram_row([b[...] for b in blocks])


def outer_kernel(step, *refs):
    first, last = step == 0, step == STEPS - 1
    blocks, refs = refs[: step + 1], refs[step + 1 :]
    if last:
        rows, refs = refs[:STEPS], refs[STEPS:]
    part_ref, e_ref, o_ref, ee_ref, oo_ref, eh_ref, el_ref, new_ref, *outs = refs
    px, py = parity()
    low = low_lanes((R, L))
    gx, gy = lax.axis_index("gx"), lax.axis_index("gy")
    o_there = jnp.logical_and(gx > 0, gx < lax.axis_size("gx") - 1)
    oo_there = jnp.logical_and(gy > 0, gy < lax.axis_size("gy") - 1)
    pairs = [[None] * Z for _ in range(2)]
    for z in range(Z):
        at = slice(z * L, (z + 1) * L)
        e, o, ee, oo = e_ref[:, at], o_ref[:, at], ee_ref[:, at], oo_ref[:, at]
        o = jnp.where(o_there, o, 0.0)
        oo = jnp.where(oo_there, oo, 0.0)
        x0, x1 = jnp.where(px == 0, o, e), jnp.where(px == 0, e, o)
        ym, yp = jnp.where(py == 0, oo, ee), jnp.where(py == 0, ee, oo)
        left0 = jnp.concatenate([jnp.where(low, ym, swapped(x0)), jnp.where(low, yp, x0)], axis=0)
        left1 = jnp.concatenate([jnp.where(low, x1, ym), jnp.where(low, swapped(x1), yp)], axis=0)
        for x, left in ((0, left0), (1, left1)):
            here = lanes(x, z)
            applied = part_ref[:, here] + product(left, eh_ref[x, z], el_ref[x, z])
            shifted = (applied - 8.0 * blocks[-1][:, here]) * (1.0 / 6.0)
            pairs[x][z] = shifted if first else 2.0 * shifted - blocks[-2][:, here]
            new_ref[:, here] = pairs[x][z]
    if not last:
        store_packets(pairs, px, py, *outs)
        return
    newest = jnp.concatenate(pairs[0] + pairs[1], axis=1)
    row4 = gram_row([b[...] for b in blocks] + [newest])
    row0, row1, row2, row3 = (r[...] for r in rows)
    outs[0][:R, :] = row4 + pltpu.roll(row2, 5 * R, 1)
    outs[0][R:, :] = row3 + pltpu.roll(row1, 4 * R, 1) + pltpu.roll(row0, 6 * R, 1)


def unpacked(g_ref):
    one, two = g_ref[:R, :], g_ref[R:, :]
    shifted = [
        pltpu.roll(two, L - 6 * R, 1),
        pltpu.roll(two, L - 4 * R, 1),
        pltpu.roll(one, L - 5 * R, 1),
        two,
        one,
    ]
    lane = lax.broadcasted_iota(jnp.int32, (R, L), 1)
    rows = [jnp.where(lane < (k + 1) * R, row, 0.0) for k, row in enumerate(shifted)]
    lower = jnp.concatenate(rows + [jnp.zeros((L - COLS, L), F32)], axis=0)
    across = jnp.transpose(lower)
    return [
        jnp.where(lane < (k + 1) * R, rows[k], across[k * R : (k + 1) * R]) for k in range(STEPS + 1)
    ]


def factor(tiles):
    n = len(tiles)
    lane = lax.broadcasted_iota(jnp.int32, (8, L), 1)
    sub = lax.broadcasted_iota(jnp.int32, (8, L), 0)

    def row(value, s):
        return jnp.broadcast_to(value[s : s + 1, :], (8, L))

    triangle, inverse = [], []
    for t in range(n):
        panel = [
            [jnp.broadcast_to(tiles[j][:, 8 * t + c : 8 * t + c + 1], (8, L)) for c in range(8)]
            for j in range(t, n)
        ]
        pivots = None
        for s in range(8):
            here = lane == 8 * t + s
            pivot = row(panel[0][s], s)
            pivots = pivot if s == 0 else jnp.where(sub == s, pivot, pivots)
            one_over = 1.0 / pivot
            scaled = jnp.where(here, 1.0, row(tiles[t], s)) * one_over
            ahead = [row(panel[0][c], s) * one_over for c in range(s + 1, 8)]
            for j in range(t, n):
                factors = panel[j - t][s]
                cleared = here
                if j == t:
                    factors = jnp.where(sub > s, factors, 0.0)
                    cleared = jnp.logical_and(here, sub > s)
                for c in range(s + 1, 8):
                    panel[j - t][c] = panel[j - t][c] - factors * ahead[c - s - 1]
                tiles[j] = jnp.where(cleared, 0.0, tiles[j]) - factors * scaled
        scale = lax.rsqrt(pivots)
        rows = tiles[t] * scale
        index = sub + 8 * t
        triangle.append(jnp.where(lane >= index, rows, 0.0))
        inverse.append(jnp.where(lane < index, rows, jnp.where(lane == index, scale, 0.0)))
    return triangle, inverse


def finish_kernel(g_ref, *refs):
    *blocks, q_ref, r_ref = refs
    tiles = [half for row in unpacked(g_ref) for half in (row[:8], row[8:])]
    triangle, inverse = factor(tiles)
    r_ref[...] = jnp.concatenate(triangle, axis=0)[:, :COLS]
    inverse = jnp.concatenate(inverse, axis=0)[:, :COLS]
    for x in range(2):
        for z in range(Z):
            tall = jnp.concatenate([b[:, lanes(x, z)] for b in blocks], axis=0)
            rows = jnp.transpose(
                jnp.dot(inverse, tall, precision=lax.Precision.HIGHEST, preferred_element_type=F32)
            )
            q_ref[x, 0, z] = rows[:U]
            q_ref[x, 1, z] = rows[U:]


def call(kernel, outs, operands):
    return pl.pallas_call(
        kernel,
        out_shape=[jax.ShapeDtypeStruct(*s) for s in outs],
        in_specs=[VM] * len(operands),
        out_specs=[VM] * len(outs),
        compiler_params=pltpu.CompilerParams(vmem_limit_bytes=VMEM_LIMIT),
    )(*operands)


BLOCK = ((R, WIDE), F32)
PACKETS = [((R, FACE), F32)] * 4
GRAM_ROW = ((R, L), F32)


def exchange(packets):
    wide = lax.axis_size("gx")
    deep = lax.axis_size("gy")

    def even(n):
        return [(i, i ^ 1) for i in range(n)]

    def odd(n):
        there = [(i, (i + 1) % n) for i in range(1, n, 2)]
        return there + [(j, i) for i, j in there]

    e, o, ee, oo = packets
    oo = lax.ppermute(oo, "gy", odd(deep))
    ee = lax.ppermute(ee, "gy", even(deep))
    o = lax.ppermute(o, "gx", odd(wide))
    e = lax.ppermute(e, "gx", even(wide))
    return e, o, ee, oo


GROUPS = ((8, 9, 1), (16 + 8, 48 + 8, 32 + 8), (64 + 8, 192 + 8, 128 + 8), (2 + 8, 6 + 8, 5 + 8))


def total_over_devices(gram):
    axes = ("gx", "gy")
    count = lax.axis_size("gx") * lax.axis_size("gy")
    for masks in GROUPS:
        a, b, c = (lax.ppermute(gram, axes, [(i, i ^ m) for i in range(count)]) for m in masks)
        gram = (gram + a) + (b + c)
    return gram


def first_product(operator_blocks, now):
    local, outer = ((2, Z, L, 3 * L), BF16), ((2, Z, L, L), BF16)
    outs = [local, local, outer, outer, BLOCK, GRAM_ROW]
    return pl.pallas_call(
        first_kernel,
        out_shape=[jax.ShapeDtypeStruct(*s) for s in outs],
        in_specs=[pl.BlockSpec(memory_space=pltpu.HBM), VM],
        out_specs=[VM] * len(outs),
        scratch_shapes=[
            pltpu.VMEM((Z, 2, 2, 7, U, U), F32),
            pltpu.SemaphoreType.DMA((Z,)),
        ],
        compiler_params=pltpu.CompilerParams(vmem_limit_bytes=VMEM_LIMIT),
    )(pltpu.with_memory_space_constraint(operator_blocks, pltpu.HBM), now)


def per_device(operator_blocks, start_block):
    start = jnp.swapaxes(start_block, 3, 4)
    now, *packets = call(begin_kernel, [BLOCK] + PACKETS, [start])
    arrived = exchange(packets)
    *weights, part, row = first_product(operator_blocks, now)
    blocks, rows = [now], [row]
    for step in range(STEPS):
        last = step == STEPS - 1
        if step > 0:
            part, row = call(local_kernel, [BLOCK, GRAM_ROW], [*weights[:2], *blocks])
            rows.append(row)
        new, *packets = call(
            functools.partial(outer_kernel, step),
            [BLOCK] + ([((2 * R, L), F32)] if last else PACKETS),
            [*blocks, *(rows if last else []), part, *arrived, *weights[2:]],
        )
        blocks.append(new)
        if not last:
            arrived = exchange(packets)
    gram = total_over_devices(packets[0])
    outs = [((2, 2, Z, U, COLS), F32), ((COLS, COLS), F32)]
    return call(finish_kernel, outs, [gram, *blocks])


def solution(mesh):
    in_specs = (P("gx", "gy", None, None, None, None), P("gx", "gy", None, None, None))
    out_specs = (P("gx", "gy", None, None, None), P())
    return jax.shard_map(
        per_device, mesh=mesh, in_specs=in_specs, out_specs=out_specs, check_vma=False
    )
```

```python
import functools

import jax
import jax.numpy as jnp
from jax import lax
from jax.experimental import pallas as pl
from jax.experimental.pallas import tpu as pltpu
from jax.sharding import PartitionSpec as P


F32 = jnp.float32
BF16 = jnp.bfloat16
Z = 12
R = 16
U = 64
L = 2 * U
FACE = Z * L
WIDE = 2 * FACE
STEPS = 4
COLS = (STEPS + 1) * R
VMEM_LIMIT = 16 * 1024 * 1024
NT = (((1,), (1,)), ((), ()))

VM = pl.BlockSpec(memory_space=pltpu.VMEM)


def low_lanes(shape):
    return lax.broadcasted_iota(jnp.int32, shape, len(shape) - 1) < U


def split(value):
    high = value.astype(BF16)
    return high, (value - high.astype(F32)).astype(BF16)


def product(high, low, weights):
    left = jnp.concatenate([high, low], axis=0)
    both = lax.dot_general(
        jnp.concatenate([left, left], axis=1), weights, NT, preferred_element_type=F32
    )
    return both[:R] + both[R:]


def swapped(pair):
    return pltpu.roll(pair, U, 1)


def parity():
    return lax.axis_index("gx") & 1, lax.axis_index("gy") & 1


def lanes(x, z):
    base = (x * Z + z) * L
    return slice(base, base + L)


def store_packets(pairs, px, py, e_ref, o_ref, ee_ref, oo_ref):
    low = low_lanes((R, L))
    for z in range(Z):
        at = slice(z * L, (z + 1) * L)
        first, second = pairs[0][z], pairs[1][z]
        e_ref[:, at] = jnp.where(px == 0, second, first)
        o_ref[:, at] = jnp.where(px == 0, first, second)
        turned = swapped(first)
        face0 = jnp.where(low, second, turned)
        face1 = jnp.where(low, turned, second)
        ee_ref[:, at] = jnp.where(py == 0, face1, face0)
        oo_ref[:, at] = jnp.where(py == 0, face0, face1)


def begin_kernel(s_ref, p_ref, h_ref, l_ref, e_ref, o_ref, ee_ref, oo_ref):
    px, py = parity()
    pairs = [[None] * Z for _ in range(2)]
    for x in range(2):
        for z in range(Z):
            pair = jnp.concatenate([s_ref[x, 0, z], s_ref[x, 1, z]], axis=1)
            p_ref[:, lanes(x, z)] = pair
            h_ref[:, lanes(x, z)], l_ref[:, lanes(x, z)] = split(pair)
            pairs[x][z] = pair
    store_packets(pairs, px, py, e_ref, o_ref, ee_ref, oo_ref)


def local_pair(h_ref, l_ref, w_ref, x, z):
    def rows(ref):
        zero = jnp.zeros((R, L), BF16)
        below = ref[:, lanes(x, z - 1)] if z > 0 else zero
        above = ref[:, lanes(x, z + 1)] if z < Z - 1 else zero
        return jnp.concatenate([ref[:, lanes(x, z)], ref[:, lanes(1 - x, z)], below, above], axis=1)

    return product(rows(h_ref), rows(l_ref), w_ref[x, z])


def gram_row(highs, lows):
    newest = jnp.concatenate([highs[-1], lows[-1]], axis=0)
    both = lax.dot_general(
        newest, jnp.concatenate(highs, axis=0), NT, preferred_element_type=F32
    ) + lax.dot_general(newest, jnp.concatenate(lows, axis=0), NT, preferred_element_type=F32)
    row = both[:R] + both[R:]
    return jnp.concatenate([row, jnp.zeros((R, L - row.shape[1]), F32)], axis=1)


CHUNK = 2
TILES = 4
OUTER = 2


def first_kernel(a_ref, h_ref, l_ref, w_ref, v_ref, out_ref, buffer, arrived):
    copies = [
        pltpu.make_async_copy(
            a_ref.at[:, :, pl.ds(z, CHUNK)], buffer.at[:, :, pl.ds(z, CHUNK)], arrived.at[z]
        )
        for z in range(0, Z, CHUNK)
    ]
    for copy in copies:
        copy.start()
    for x in range(2):
        for z in range(Z):
            for k in range(2):
                w_ref[x, z, :, (k * TILES + 1) * L : (k + 1) * TILES * L] = jnp.zeros(
                    (L, (TILES - 1) * L), BF16
                )
            v_ref[x, z] = jnp.zeros((L, 2 * OUTER * L), BF16)

    def store(ref, x, z, rows, tile, tiles, halves, at=slice(0, L)):
        for k, half in enumerate(halves):
            base = (k * tiles + tile) * L
            ref[x, z, rows, base + at.start : base + at.stop] = half[:, at]

    def multiply(chunk):
        for z in chunk:
            for x in range(2):
                out_ref[:, lanes(x, z)] = local_pair(h_ref, l_ref, w_ref, x, z)

    behind = ()
    for z0, copy in zip(range(0, Z, CHUNK), copies):
        copy.wait()
        chunk = range(z0, z0 + CHUNK)
        for z in chunk:
            for x in range(2):
                rows = (slice(0, U), slice(U, L))

                def block(y, f):
                    return buffer[x, y, z, f]

                def beside(one, two):
                    return split(jnp.concatenate([one, two], axis=1))

                store(w_ref, x, z, rows[0], 0, TILES, beside(block(0, 0), block(0, 4)))
                store(w_ref, x, z, rows[1], 0, TILES, beside(block(1, 3), block(1, 0)))
                apart = [
                    (w_ref, 1, TILES, 2 - x, 2 - x),
                    (w_ref, 2, TILES, 5, 5),
                    (w_ref, 3, TILES, 6, 6),
                    (v_ref, 0, OUTER, 1 + x, 1 + x),
                    (v_ref, 1, OUTER, 3, 4),
                ]
                for ref, tile, tiles, fa, fb in apart:
                    turn = x if ref is v_ref and tile == 1 else 0
                    one, two = block(0, fa), block(1, fb)
                    halves = beside(two, one) if turn else beside(one, two)
                    store(ref, x, z, rows[turn], tile, tiles, halves, rows[0])
                    store(ref, x, z, rows[1 - turn], tile, tiles, halves, rows[1])
        multiply(behind)
        behind = chunk
    multiply(behind)


def local_kernel(step, w_ref, *refs):
    highs, lows = refs[: step + 1], refs[step + 1 : 2 * step + 2]
    out_ref, *rows = refs[2 * step + 2 :]
    if step == 1:
        rows[0][...] = gram_row([h[...] for h in highs[:1]], [l[...] for l in lows[:1]])
    rows[-1][...] = gram_row([h[...] for h in highs], [l[...] for l in lows])
    for z in range(Z):
        for x in range(2):
            out_ref[:, lanes(x, z)] = local_pair(highs[-1], lows[-1], w_ref, x, z)


def outer_kernel(step, *refs):
    first, last = step == 0, step == STEPS - 1
    now_ref, refs = refs[0], refs[1:]
    if not first:
        before_ref, refs = refs[0], refs[1:]
    if last:
        rows, highs, lows = refs[:STEPS], refs[STEPS : 2 * STEPS], refs[2 * STEPS : 3 * STEPS]
        refs = refs[3 * STEPS :]
    part_ref, e_ref, o_ref, ee_ref, oo_ref, v_ref, *outs = refs
    high_ref, low_ref, *outs = outs
    px, py = parity()
    low = low_lanes((R, L))
    gx, gy = lax.axis_index("gx"), lax.axis_index("gy")
    o_there = jnp.logical_and(gx > 0, gx < lax.axis_size("gx") - 1)
    oo_there = jnp.logical_and(gy > 0, gy < lax.axis_size("gy") - 1)
    pairs, sums = [[None] * Z for _ in range(2)], []
    for z in range(Z):
        at = slice(z * L, (z + 1) * L)
        e, o, ee, oo = e_ref[:, at], o_ref[:, at], ee_ref[:, at], oo_ref[:, at]
        o = jnp.where(o_there, o, 0.0)
        oo = jnp.where(oo_there, oo, 0.0)
        x0, x1 = jnp.where(px == 0, o, e), jnp.where(px == 0, e, o)
        ym, yp = jnp.where(py == 0, oo, ee), jnp.where(py == 0, ee, oo)
        beyond = ((x0, jnp.where(low, ym, yp)), (x1, jnp.where(low, yp, ym)))
        for x, left in enumerate(beyond):
            here = lanes(x, z)
            high, less = split(jnp.concatenate(left, axis=1))
            applied = part_ref[:, here] + product(high, less, v_ref[x, z])
            shifted = (applied - 8.0 * now_ref[:, here]) * (1.0 / 6.0)
            pairs[x][z] = shifted if first else 2.0 * shifted - before_ref[:, here]
            high_ref[:, here], low_ref[:, here] = split(pairs[x][z])
            if not last:
                outs[0][:, here] = pairs[x][z]
            else:
                newest = [high_ref[:, here], low_ref[:, here]]
                every = [h[:, here] for h in highs] + newest[:1] + [l[:, here] for l in lows] + newest[1:]
                sums.append((jnp.concatenate(newest, axis=0), jnp.concatenate(every, axis=0)))
    if not last:
        store_packets(pairs, px, py, *outs[1:])
        return
    both = jnp.zeros((2 * R, 2 * COLS), F32)
    for one, two in zip(sums[::2], sums[1::2]):
        newest, every = (jnp.concatenate(half, axis=1) for half in zip(one, two))
        both = both + lax.dot_general(newest, every, NT, preferred_element_type=F32)
    both = both[:R] + both[R:]
    row4 = jnp.concatenate([both[:, :COLS] + both[:, COLS:], jnp.zeros((R, L - COLS), F32)], axis=1)
    row0, row1, row2, row3 = (r[...] for r in rows)
    outs[0][:R, :] = row4 + pltpu.roll(row2, 5 * R, 1)
    outs[0][R:, :] = row3 + pltpu.roll(row1, 4 * R, 1) + pltpu.roll(row0, 6 * R, 1)


def unpacked(g_ref):
    one, two = g_ref[:R, :], g_ref[R:, :]
    shifted = [
        pltpu.roll(two, L - 6 * R, 1),
        pltpu.roll(two, L - 4 * R, 1),
        pltpu.roll(one, L - 5 * R, 1),
        two,
        one,
    ]
    lane = lax.broadcasted_iota(jnp.int32, (R, L), 1)
    rows = [jnp.where(lane < (k + 1) * R, row, 0.0) for k, row in enumerate(shifted)]
    lower = jnp.concatenate(rows + [jnp.zeros((L - COLS, L), F32)], axis=0)
    across = jnp.transpose(lower)
    return [
        jnp.where(lane < (k + 1) * R, rows[k], across[k * R : (k + 1) * R]) for k in range(STEPS + 1)
    ]


def factor(tiles):
    n = len(tiles)
    lane = lax.broadcasted_iota(jnp.int32, (8, L), 1)
    sub = lax.broadcasted_iota(jnp.int32, (8, L), 0)

    def row(value, s):
        return jnp.broadcast_to(value[s : s + 1, :], (8, L))

    triangle, inverse = [], []
    for t in range(n):
        base = 8 * t
        panel = [
            [jnp.broadcast_to(tiles[j][:, base + c : base + c + 1], (8, L)) for c in range(8)]
            for j in range(t, n)
        ]
        inside = jnp.logical_and(lane >= base, lane < base + 8)
        tiles[t] = jnp.where(inside, jnp.where(lane - base == sub, 1.0, 0.0), tiles[t])
        for j in range(t + 1, n):
            tiles[j] = jnp.where(inside, 0.0, tiles[j])
        pivots = None
        for s in range(8):
            pivot = row(panel[0][s], s)
            pivots = pivot if s == 0 else jnp.where(sub == s, pivot, pivots)
            one_over = 1.0 / pivot
            scaled = row(tiles[t], s) * one_over
            ahead = [row(panel[0][c], s) * one_over for c in range(s + 1, 8)]
            for j in range(t, n):
                factors = panel[j - t][s]
                if j == t:
                    factors = jnp.where(sub > s, factors, 0.0)
                for c in range(s + 1, 8):
                    panel[j - t][c] = panel[j - t][c] - factors * ahead[c - s - 1]
                tiles[j] = tiles[j] - factors * scaled
        scale = lax.rsqrt(pivots)
        rows = tiles[t] * scale
        inverse.append(jnp.where(lane < base + 8, rows, 0.0))
        rows = jnp.where(lane < base + 8, 0.0, rows)
        for c in range(8):
            here = jnp.logical_and(lane == base + c, sub <= c)
            rows = jnp.where(here, panel[0][c] * scale, rows)
        triangle.append(rows)
    return triangle, inverse


def finish_kernel(g_ref, *refs):
    count = STEPS + 1
    highs, lows, (q_ref, r_ref) = refs[:count], refs[count : 2 * count], refs[2 * count :]
    tiles = [half for row in unpacked(g_ref) for half in (row[:8], row[8:])]
    triangle, inverse = factor(tiles)
    r_ref[...] = jnp.concatenate(triangle, axis=0)[:, :COLS]
    inverse = jnp.concatenate(inverse, axis=0)[:, :COLS]
    high, low = (half.astype(F32) for half in split(inverse))
    left = jnp.concatenate([high, high, low], axis=1).astype(BF16)
    for x in range(2):
        for z in range(Z):
            here = lanes(x, z)
            high = [h[:, here] for h in highs]
            low = [l[:, here] for l in lows]
            right = jnp.concatenate(high + low + high, axis=0)
            rows = jnp.transpose(jnp.dot(left, right, preferred_element_type=F32))
            q_ref[x, 0, z] = rows[:U]
            q_ref[x, 1, z] = rows[U:]


def call(kernel, outs, operands, **more):
    return pl.pallas_call(
        kernel,
        out_shape=[jax.ShapeDtypeStruct(*s) for s in outs],
        in_specs=more.pop("in_specs", [VM] * len(operands)),
        out_specs=more.pop("out_specs", [VM] * len(outs)),
        compiler_params=pltpu.CompilerParams(vmem_limit_bytes=VMEM_LIMIT),
        **more,
    )(*operands)


BLOCK = ((R, WIDE), F32)
HALVES = [((R, WIDE), BF16)] * 2
PACKETS = [((R, FACE), F32)] * 4
GRAM_ROW = ((R, L), F32)


def exchange(packets):
    wide = lax.axis_size("gx")
    deep = lax.axis_size("gy")

    def even(n):
        return [(i, i ^ 1) for i in range(n)]

    def odd(n):
        there = [(i, (i + 1) % n) for i in range(1, n, 2)]
        return there + [(j, i) for i, j in there]

    e, o, ee, oo = packets
    oo = lax.ppermute(oo, "gy", odd(deep))
    ee = lax.ppermute(ee, "gy", even(deep))
    o = lax.ppermute(o, "gx", odd(wide))
    e = lax.ppermute(e, "gx", even(wide))
    return e, o, ee, oo


GROUPS = ((8, 9, 1), (16 + 8, 48 + 8, 32 + 8), (64 + 8, 192 + 8, 128 + 8), (2 + 8, 6 + 8, 5 + 8))


def total_over_devices(gram):
    axes = ("gx", "gy")
    count = lax.axis_size("gx") * lax.axis_size("gy")
    for masks in GROUPS:
        terms = [lax.ppermute(gram, axes, [(i, i ^ m) for i in range(count)]) for m in masks]
        gram = gram + terms[0]
        if len(masks) == 3:
            gram = gram + (terms[1] + terms[2])
    return gram


def first_product(operator_blocks, high, low):
    return call(
        first_kernel,
        [((2, Z, L, 2 * TILES * L), BF16), ((2, Z, L, 2 * OUTER * L), BF16), BLOCK],
        [pltpu.with_memory_space_constraint(operator_blocks, pltpu.HBM), high, low],
        in_specs=[pl.BlockSpec(memory_space=pltpu.HBM), VM, VM],
        scratch_shapes=[pltpu.VMEM((2, 2, Z, 7, U, U), F32), pltpu.SemaphoreType.DMA((Z,))],
    )


def per_device(operator_blocks, start_block):
    start = jnp.swapaxes(start_block, 3, 4)
    now, high, low, *packets = call(begin_kernel, [BLOCK] + HALVES + PACKETS, [start])
    arrived = exchange(packets)
    local, outer, part = first_product(operator_blocks, high, low)
    recent, highs, lows, rows = [now], [high], [low], []
    for step in range(STEPS):
        last = step == STEPS - 1
        if step > 0:
            part, *new_rows = call(
                functools.partial(local_kernel, step),
                [BLOCK] + [GRAM_ROW] * (2 if step == 1 else 1),
                [local, *highs, *lows],
            )
            rows += new_rows
        high, low, *outs = call(
            functools.partial(outer_kernel, step),
            HALVES + ([((2 * R, L), F32)] if last else [BLOCK] + PACKETS),
            [*recent, *(rows + highs + lows if last else []), part, *arrived, outer],
        )
        highs.append(high)
        lows.append(low)
        if not last:
            recent = [outs[0], recent[0]]
            arrived = exchange(outs[1:])
    gram = total_over_devices(outs[0])
    return call(
        finish_kernel,
        [((2, 2, Z, U, COLS), F32), ((COLS, COLS), F32)],
        [gram, *highs, *lows],
    )


def solution(mesh):
    in_specs = (P("gx", "gy", None, None, None, None), P("gx", "gy", None, None, None))
    out_specs = (P("gx", "gy", None, None, None), P())
    return jax.shard_map(
        per_device, mesh=mesh, in_specs=in_specs, out_specs=out_specs, check_vma=False
    )
```

```python
import functools

import jax
import jax.numpy as jnp
from jax import lax
from jax.experimental import pallas as pl
from jax.experimental.pallas import tpu as pltpu
from jax.sharding import PartitionSpec as P


F32 = jnp.float32
BF16 = jnp.bfloat16
Z = 12
R = 16
U = 64
L = 2 * U
FACE = Z * L
WIDE = 2 * FACE
STEPS = 4
COLS = (STEPS + 1) * R
VMEM_LIMIT = 16 * 1024 * 1024
NT = (((1,), (1,)), ((), ()))

VM = pl.BlockSpec(memory_space=pltpu.VMEM)


def low_lanes(shape):
    return lax.broadcasted_iota(jnp.int32, shape, len(shape) - 1) < U


def split(value):
    high = value.astype(BF16)
    return high, (value - high.astype(F32)).astype(BF16)


def product(one, two, weights):
    same = one is two
    left = jnp.concatenate([one[0], one[1]] if same else [one[0], two[0], one[1], two[1]], axis=0)
    both = lax.dot_general(
        jnp.concatenate([left, left], axis=1), weights, NT, preferred_element_type=F32
    )
    count = both.shape[0] // 2
    both = both[:count] + both[count:]
    return both if same else jnp.where(low_lanes((R, L)), both[:R], both[R:])


def swapped(pair):
    return pltpu.roll(pair, U, 1)


def parity():
    return lax.axis_index("gx") & 1, lax.axis_index("gy") & 1


def lanes(x, z):
    base = (x * Z + z) * L
    return slice(base, base + L)


def store_packets(pairs, px, py, e_ref, o_ref, ee_ref, oo_ref):
    low = low_lanes((R, L))
    for z in range(Z):
        at = slice(z * L, (z + 1) * L)
        first, second = pairs[0][z], pairs[1][z]
        e_ref[:, at] = jnp.where(px == 0, second, first)
        o_ref[:, at] = jnp.where(px == 0, first, second)
        turned = swapped(first)
        face0 = jnp.where(low, second, turned)
        face1 = jnp.where(low, turned, second)
        ee_ref[:, at] = jnp.where(py == 0, face1, face0)
        oo_ref[:, at] = jnp.where(py == 0, face0, face1)


def begin_kernel(s_ref, p_ref, h_ref, l_ref, e_ref, o_ref, ee_ref, oo_ref):
    px, py = parity()
    pairs = [[None] * Z for _ in range(2)]
    for x in range(2):
        for z in range(Z):
            pair = jnp.concatenate([s_ref[x, 0, z], s_ref[x, 1, z]], axis=1)
            p_ref[:, lanes(x, z)] = pair
            h_ref[x, z], l_ref[x, z] = split(pair)
            pairs[x][z] = pair
    store_packets(pairs, px, py, e_ref, o_ref, ee_ref, oo_ref)


def local_pairs(h_ref, l_ref, w_ref):
    low = lax.broadcasted_iota(jnp.int32, (R, L), 1).astype(F32).astype(BF16) < U
    zero = jnp.zeros((R, L), BF16)

    made = {}

    def left(k, x, z):
        ref = (h_ref, l_ref)[k]

        def turned(x, z):
            if (k, x, z) not in made:
                made[k, x, z] = swapped(ref[x, z].astype(F32)).astype(BF16)
            return made[k, x, z]

        below, above = z > 0, z < Z - 1
        here = ref[x, z]
        first = jnp.where(
            low, ref[x, z - 1] if below else zero, turned(x, z + 1) if above else zero
        )
        second = jnp.where(
            low, turned(x, z - 1) if below else zero, ref[x, z + 1] if above else zero
        )
        return [jnp.concatenate([here, v, ref[1 - x, z]], axis=1) for v in (first, second)]

    def pair(x, z):
        (first_h, second_h), (first_l, second_l) = left(0, x, z), left(1, x, z)
        weights = jnp.concatenate([w_ref[x, z, k] for k in range(2 * TILES)], axis=1)
        return product((first_h, first_l), (second_h, second_l), weights)

    return pair


def wide(ref):
    return jnp.concatenate([ref[x, z] for x in range(2) for z in range(Z)], axis=1)


def gram_row(highs, lows):
    newest = jnp.concatenate([highs[-1], lows[-1]], axis=0)
    both = lax.dot_general(
        newest, jnp.concatenate(highs, axis=0), NT, preferred_element_type=F32
    ) + lax.dot_general(newest, jnp.concatenate(lows, axis=0), NT, preferred_element_type=F32)
    row = both[:R] + both[R:]
    return jnp.concatenate([row, jnp.zeros((R, L - row.shape[1]), F32)], axis=1)


CHUNK = 2
TILES = 3
OUTER = 2


def first_kernel(a_ref, h_ref, l_ref, w_ref, v_ref, out_ref, buffer, arrived):
    copies = [
        pltpu.make_async_copy(
            a_ref.at[:, :, pl.ds(z, CHUNK)], buffer.at[:, :, pl.ds(z, CHUNK)], arrived.at[z]
        )
        for z in range(0, Z, CHUNK)
    ]
    for copy in copies:
        copy.start()
    low_half = low_lanes((U, L))

    def store(ref, x, z, rows, tile, tiles, halves):
        for k, half in enumerate(halves):
            at = k * tiles + tile
            if ref is w_ref:
                ref[x, z, at, rows, :] = half
            else:
                ref[x, z, rows, at * L : (at + 1) * L] = half

    pair = local_pairs(h_ref, l_ref, w_ref)

    def multiply(chunk):
        for z in chunk:
            for x in range(2):
                out_ref[:, lanes(x, z)] = pair(x, z)

    behind = ()
    for z0, copy in zip(range(0, Z, CHUNK), copies):
        copy.wait()
        chunk = range(z0, z0 + CHUNK)
        for z in chunk:
            for x in range(2):
                rows = (slice(0, U), slice(U, L))

                def block(y, f):
                    return buffer[x, y, z, f]

                def beside(one, two):
                    return split(jnp.concatenate([one, two], axis=1))

                store(w_ref, x, z, rows[0], 0, TILES, beside(block(0, 0), block(0, 4)))
                store(w_ref, x, z, rows[1], 0, TILES, beside(block(1, 3), block(1, 0)))
                for y in range(2):
                    store(w_ref, x, z, rows[y], 1, TILES, beside(block(y, 5), block(y, 6)))
                apart = [
                    (w_ref, 2, TILES, 2 - x, 2 - x, 0),
                    (v_ref, 0, OUTER, 1 + x, 1 + x, 0),
                    (v_ref, 1, OUTER, 3, 4, x),
                ]
                for ref, tile, tiles, fa, fb, turn in apart:
                    one, two = block(0, fa), block(1, fb)
                    both = jnp.concatenate([two, one] if turn else [one, two], axis=1)
                    lower = split(jnp.where(low_half, both, 0.0))
                    upper = split(jnp.where(low_half, 0.0, both))
                    store(ref, x, z, rows[turn], tile, tiles, lower)
                    store(ref, x, z, rows[1 - turn], tile, tiles, upper)
        multiply(behind)
        behind = chunk
    multiply(behind)


def local_kernel(step, w_ref, *refs):
    highs, lows = refs[: step + 1], refs[step + 1 : 2 * step + 2]
    out_ref, *rows = refs[2 * step + 2 :]
    if step == 1:
        rows[0][...] = gram_row([wide(highs[0])], [wide(lows[0])])
    rows[-1][...] = gram_row([wide(h) for h in highs], [wide(l) for l in lows])
    pair = local_pairs(highs[-1], lows[-1], w_ref)
    for z in range(Z):
        for x in range(2):
            out_ref[:, lanes(x, z)] = pair(x, z)


def outer_kernel(step, *refs):
    first, last = step == 0, step == STEPS - 1
    now_ref, refs = refs[0], refs[1:]
    if not first:
        before_ref, refs = refs[0], refs[1:]
    if last:
        rows, highs, lows = refs[:STEPS], refs[STEPS : 2 * STEPS], refs[2 * STEPS : 3 * STEPS]
        refs = refs[3 * STEPS :]
    part_ref, e_ref, o_ref, ee_ref, oo_ref, v_ref, *outs = refs
    high_ref, low_ref, *outs = outs
    px, py = parity()
    low = low_lanes((R, L))
    gx, gy = lax.axis_index("gx"), lax.axis_index("gy")
    o_there = jnp.logical_and(gx > 0, gx < lax.axis_size("gx") - 1)
    oo_there = jnp.logical_and(gy > 0, gy < lax.axis_size("gy") - 1)
    pairs, sums = [[None] * Z for _ in range(2)], []
    for z in range(Z):
        at = slice(z * L, (z + 1) * L)
        e, o, ee, oo = e_ref[:, at], o_ref[:, at], ee_ref[:, at], oo_ref[:, at]
        o = jnp.where(o_there, o, 0.0)
        oo = jnp.where(oo_there, oo, 0.0)
        x0, x1 = jnp.where(px == 0, o, e), jnp.where(px == 0, e, o)
        ym, yp = jnp.where(py == 0, oo, ee), jnp.where(py == 0, ee, oo)
        beyond = ((x0, jnp.where(low, ym, yp)), (x1, jnp.where(low, yp, ym)))
        for x, left in enumerate(beyond):
            here = lanes(x, z)
            left = split(jnp.concatenate(left, axis=1))
            applied = part_ref[:, here] + product(left, left, v_ref[x, z])
            shifted = (applied - 8.0 * now_ref[:, here]) * (1.0 / 6.0)
            pairs[x][z] = shifted if first else 2.0 * shifted - before_ref[:, here]
            high_ref[x, z], low_ref[x, z] = split(pairs[x][z])
            if not last:
                outs[0][:, here] = pairs[x][z]
            else:
                newest = [high_ref[x, z], low_ref[x, z]]
                every = [h[x, z] for h in highs] + newest[:1] + [l[x, z] for l in lows] + newest[1:]
                sums.append((jnp.concatenate(newest, axis=0), jnp.concatenate(every, axis=0)))
    if not last:
        store_packets(pairs, px, py, *outs[1:])
        return
    both = jnp.zeros((2 * R, 2 * COLS), F32)
    for one, two in zip(sums[::2], sums[1::2]):
        newest, every = (jnp.concatenate(half, axis=1) for half in zip(one, two))
        both = both + lax.dot_general(newest, every, NT, preferred_element_type=F32)
    both = both[:R] + both[R:]
    row4 = jnp.concatenate([both[:, :COLS] + both[:, COLS:], jnp.zeros((R, L - COLS), F32)], axis=1)
    row0, row1, row2, row3 = (r[...] for r in rows)
    outs[0][:R, :] = row4 + pltpu.roll(row2, 5 * R, 1)
    outs[0][R:, :] = row3 + pltpu.roll(row1, 4 * R, 1) + pltpu.roll(row0, 6 * R, 1)


def unpacked(g_ref):
    one, two = g_ref[:R, :], g_ref[R:, :]
    shifted = [
        pltpu.roll(two, L - 6 * R, 1),
        pltpu.roll(two, L - 4 * R, 1),
        pltpu.roll(one, L - 5 * R, 1),
        two,
        one,
    ]
    lane = lax.broadcasted_iota(jnp.int32, (R, L), 1)
    rows = [jnp.where(lane < (k + 1) * R, row, 0.0) for k, row in enumerate(shifted)]
    lower = jnp.concatenate(rows + [jnp.zeros((L - COLS, L), F32)], axis=0)
    across = jnp.transpose(lower)
    return [
        jnp.where(lane < (k + 1) * R, rows[k], across[k * R : (k + 1) * R]) for k in range(STEPS + 1)
    ]


def factor(tiles):
    n = len(tiles)
    lane = lax.broadcasted_iota(jnp.int32, (8, L), 1)
    sub = lax.broadcasted_iota(jnp.int32, (8, L), 0)

    def row(value, s):
        return jnp.broadcast_to(value[s : s + 1, :], (8, L))

    triangle, inverse = [], []
    for t in range(n):
        base = 8 * t
        panel = [
            [jnp.broadcast_to(tiles[j][:, base + c : base + c + 1], (8, L)) for c in range(8)]
            for j in range(t, n)
        ]
        inside = jnp.logical_and(lane >= base, lane < base + 8)
        tiles[t] = jnp.where(inside, jnp.where(lane - base == sub, 1.0, 0.0), tiles[t])
        for j in range(t + 1, n):
            tiles[j] = jnp.where(inside, 0.0, tiles[j])
        pivots = pivot = row(panel[0][0], 0)
        for s in range(8):
            pivots = jnp.where(sub == s, pivot, pivots)
            one_over = 1.0 / pivot
            scaled = row(tiles[t], s) * one_over
            across = [row(panel[0][c], s) for c in range(s + 1, 8)]
            ahead = [value * one_over for value in across]
            if s < 7:
                pivot = row(panel[0][s + 1], s + 1) - across[0] * ahead[0]
            for j in range(t, n):
                factors = panel[j - t][s]
                if j == t:
                    factors = jnp.where(sub > s, factors, 0.0)
                for c in range(s + 1, 8):
                    panel[j - t][c] = panel[j - t][c] - factors * ahead[c - s - 1]
                tiles[j] = tiles[j] - factors * scaled
        scale = lax.rsqrt(pivots)
        rows = tiles[t] * scale
        inverse.append(jnp.where(lane < base + 8, rows, 0.0))
        rows = jnp.where(lane < base + 8, 0.0, rows)
        for c in range(8):
            here = jnp.logical_and(lane == base + c, sub <= c)
            rows = jnp.where(here, panel[0][c] * scale, rows)
        triangle.append(rows)
    return triangle, inverse


def finish_kernel(g_ref, *refs):
    count = STEPS + 1
    highs, lows, (q_ref, r_ref) = refs[:count], refs[count : 2 * count], refs[2 * count :]
    tiles = [half for row in unpacked(g_ref) for half in (row[:8], row[8:])]
    triangle, inverse = factor(tiles)
    r_ref[...] = jnp.concatenate(triangle, axis=0)[:, :COLS]
    inverse = jnp.concatenate(inverse, axis=0)[:, :COLS]
    high, low = (half.astype(F32) for half in split(inverse))
    left = jnp.concatenate([high, high, low], axis=1).astype(BF16)
    for x in range(2):
        for z in range(Z):
            high = [h[x, z] for h in highs]
            low = [l[x, z] for l in lows]
            right = jnp.concatenate(high + low + high, axis=0)
            rows = jnp.transpose(jnp.dot(left, right, preferred_element_type=F32))
            q_ref[x, 0, z] = rows[:U]
            q_ref[x, 1, z] = rows[U:]


def call(kernel, outs, operands, **more):
    return pl.pallas_call(
        kernel,
        out_shape=[jax.ShapeDtypeStruct(*s) for s in outs],
        in_specs=more.pop("in_specs", [VM] * len(operands)),
        out_specs=more.pop("out_specs", [VM] * len(outs)),
        compiler_params=pltpu.CompilerParams(vmem_limit_bytes=VMEM_LIMIT),
        **more,
    )(*operands)


BLOCK = ((R, WIDE), F32)
HALVES = [((2, Z, R, L), BF16)] * 2
PACKETS = [((R, FACE), F32)] * 4
GRAM_ROW = ((R, L), F32)


def exchange(packets):
    wide = lax.axis_size("gx")
    deep = lax.axis_size("gy")

    def even(n):
        return [(i, i ^ 1) for i in range(n)]

    def odd(n):
        there = [(i, (i + 1) % n) for i in range(1, n, 2)]
        return there + [(j, i) for i, j in there]

    e, o, ee, oo = packets
    oo = lax.ppermute(oo, "gy", odd(deep))
    ee = lax.ppermute(ee, "gy", even(deep))
    o = lax.ppermute(o, "gx", odd(wide))
    e = lax.ppermute(e, "gx", even(wide))
    return e, o, ee, oo


GROUPS = ((8,), (16 + 8, 48 + 8, 32 + 8), (64 + 8, 192 + 8, 128 + 8), (1 + 8, 2 + 8, 3 + 8), (7 + 8,))


def total_over_devices(gram):
    axes = ("gx", "gy")
    count = lax.axis_size("gx") * lax.axis_size("gy")
    for masks in GROUPS:
        terms = [lax.ppermute(gram, axes, [(i, i ^ m) for i in range(count)]) for m in masks]
        gram = gram + terms[0]
        if len(masks) == 3:
            gram = gram + (terms[1] + terms[2])
    return gram


def first_product(operator_blocks, high, low):
    return call(
        first_kernel,
        [((2, Z, 2 * TILES, L, L), BF16), ((2, Z, L, 2 * OUTER * L), BF16), BLOCK],
        [pltpu.with_memory_space_constraint(operator_blocks, pltpu.HBM), high, low],
        in_specs=[pl.BlockSpec(memory_space=pltpu.HBM), VM, VM],
        scratch_shapes=[pltpu.VMEM((2, 2, Z, 7, U, U), F32), pltpu.SemaphoreType.DMA((Z,))],
    )


def per_device(operator_blocks, start_block):
    start = jnp.swapaxes(start_block, 3, 4)
    now, high, low, *packets = call(begin_kernel, [BLOCK] + HALVES + PACKETS, [start])
    arrived = exchange(packets)
    local, outer, part = first_product(operator_blocks, high, low)
    recent, highs, lows, rows = [now], [high], [low], []
    for step in range(STEPS):
        last = step == STEPS - 1
        if step > 0:
            part, *new_rows = call(
                functools.partial(local_kernel, step),
                [BLOCK] + [GRAM_ROW] * (2 if step == 1 else 1),
                [local, *highs, *lows],
            )
            rows += new_rows
        high, low, *outs = call(
            functools.partial(outer_kernel, step),
            HALVES + ([((2 * R, L), F32)] if last else [BLOCK] + PACKETS),
            [*recent, *(rows + highs + lows if last else []), part, *arrived, outer],
        )
        highs.append(high)
        lows.append(low)
        if not last:
            recent = [outs[0], recent[0]]
            arrived = exchange(outs[1:])
    gram = total_over_devices(outs[0])
    return call(
        finish_kernel,
        [((2, 2, Z, U, COLS), F32), ((COLS, COLS), F32)],
        [gram, *highs, *lows],
    )


def solution(mesh):
    in_specs = (P("gx", "gy", None, None, None, None), P("gx", "gy", None, None, None))
    out_specs = (P("gx", "gy", None, None, None), P())
    return jax.shard_map(
        per_device, mesh=mesh, in_specs=in_specs, out_specs=out_specs, check_vma=False
    )
```
